32 devices in a mesh: grp: 2 (over x), row: 8 (over z, y), col: 2 (over core).
Axes of the slice: x: 2, y: 2, z: 4, core: 2. Of those that a mesh axis runs over, the one named last changes fastest.
Arguments:
- queries: bfloat16 [8192, 2048], P(('grp', 'row'), 'col'), parts along dimension 0, may hold values from -34 to 34
- keys: bfloat16 [8192, 1024], P(('grp', 'row'), 'col'), parts along dimension 0, may hold values from -34 to 34
- values: bfloat16 [8192, 1024], P(('grp', 'row'), 'col'), parts along dimension 0, may hold values from -6 to 6
- out_proj: bfloat16 [2048, 5376], P(('col', 'row'))
- post_gain: float32 [5376], P('col'), may hold values from 0.1 to 1.9
- mean_vec: float32 [5376], P('col'), may hold values from -5 to 5
- erase_in: float32 [5376, 64], P('col'), may hold values from -0.078125 to 0.078125
- erase_out: float32 [5376, 64], P('col'), may hold values from -0.375 to 0.375
Outputs:
- erased: bfloat16 [8192, 5376], P(('grp', 'row'), 'col'), parts along dimension 0
The draws below stay inside these ranges and needn't reach their ends.
There are 2 independent parts, one for each index of `grp`. The reference program is written for one: setup_inputs(seed, part) draws one part's arguments, and reference() takes and returns one part's arrays. A program takes and returns all parts, laid end to end along the dimension named above; an argument that names none is the same for every part. Nothing has to cross between parts.
All inputs are finite; a program needn't handle non-finite values.
Results may differ from the reference program's by a relative error of at most 0.012.
The reference program's roundings to bfloat16 on the way (of `q_rot`, `k_rot`, `probs` and `attended`) count: a program that leaves them out, or rounds other values in their place, can miss the bound.
Values may be sent and summed in bfloat16 or wider, within the bound.
A program may use at most 128 MiB of HBM per device.

```python
import jax
import jax.numpy as jnp
from jax import lax

D = 5376
HD = 128
HEADS = 16
KV = 8
WINDOW = 1024
RANK = 64
TOK_DEV = 512
TOKENS = 4096
N_ROW = 8


def base_field(key, shape):
    return jnp.clip(jax.random.normal(key, shape, jnp.float32), -4.0, 4.0)


def draw_queries(key, part):
    base_draw = base_field(jax.random.fold_in(key, 11), (TOKENS, HEADS, HD))
    return base_draw.reshape(TOKENS, HEADS * HD).astype(jnp.bfloat16)


def draw_keys(key, part):
    base_draw = base_field(jax.random.fold_in(key, 13), (TOKENS, KV, HD))
    return base_draw.reshape(TOKENS, KV * HD).astype(jnp.bfloat16)


def draw_out_proj(key, part):
    columns = jnp.arange(D).astype(jnp.float32)
    ramp = jnp.exp(jnp.log(3.0) * columns / D)
    base_draw = jnp.clip(jax.random.normal(jax.random.fold_in(key, 5), (HEADS * HD, D), jnp.float32), -5.0, 5.0)
    scaled = base_draw * ramp[None, :] * float(HEADS * HD) ** (-0.5) / 1.8
    return scaled.astype(jnp.bfloat16)


def shard_levels(key, extent, pieces, smallest, top_value):
    level = 1.0
    for axis_at, shards_of in pieces:
        steps = jax.random.uniform(jax.random.fold_in(jax.random.fold_in(key, 6), axis_at), (shards_of,), jnp.float32, smallest / len(pieces), top_value / len(pieces))
        level = level * jnp.repeat(jnp.exp(steps), extent[axis_at] // shards_of).reshape((-1,) + (1,) * (len(extent) - 1 - axis_at))
    return level


def centred(rng, shape, scale, reach, shards=(), kind=jnp.bfloat16):
    values = scale * jax.random.normal(rng, shape, jnp.float32)
    if shards:
        values = values * shard_levels(rng, shape, shards, -0.22, 0.18)
    return jnp.clip(values, -reach, reach).astype(kind)


def setup_inputs(seed: int = 0, part: int = 0) -> dict:
    splits = jax.random.split(jax.random.key(seed), 9)
    part_keys = jax.random.split(jax.random.fold_in(splits[8], part), 9)
    return {
        "queries": draw_queries(jax.random.fold_in(jax.random.fold_in(splits[8], part), 71), part),
        "keys": draw_keys(jax.random.fold_in(jax.random.fold_in(splits[8], part), 71), part),
        "values": centred(part_keys[2], (TOKENS, KV * HD), 1.0, 6.0, ((0, 8), (1, 2))),
        "out_proj": draw_out_proj(jax.random.fold_in(splits[8], 71), part),
        "post_gain": jnp.clip(1.0 + 0.18 * jax.random.normal(splits[4], (D,), jnp.float32), 0.1, 1.9),
        "mean_vec": centred(splits[5], (D,), 1.0, 5.0, ((0, 2),), jnp.float32),
        "erase_in": centred(splits[6], (D, RANK), D ** -0.5, 0.078125, ((0, 2),), jnp.float32),
        "erase_out": centred(splits[7], (D, RANK), (4 * RANK) ** -0.5, 0.375, ((0, 2),), jnp.float32),
    }


query_scale = 168.0 ** (-0.5)
norm_eps = 1e-06
rope_base = 10000.0

def rotate(field, positions):
    half_dim = HD // 2
    inverse = jnp.exp(-(2.0 * jnp.arange(half_dim, dtype=jnp.float32) / HD) * jnp.log(jnp.float32(rope_base)))
    angles = positions[:, None] * inverse[None, :]
    cosine = jnp.cos(angles)[:, None, :]
    sine = jnp.sin(angles)[:, None, :]
    wide = field.astype(jnp.float32)
    first = wide[..., :half_dim]
    second = wide[..., half_dim:]
    return jnp.concatenate([first * cosine - second * sine, second * cosine + first * sine], -1).astype(jnp.bfloat16)

def reference(queries, keys, values, out_proj, post_gain, mean_vec, erase_in, erase_out):
    group = HEADS // KV
    positions = jnp.arange(TOKENS).astype(jnp.float32)
    q_rot = rotate(queries.reshape(TOKENS, HEADS, HD), positions)
    k_rot = rotate(keys.reshape(TOKENS, KV, HD), positions)
    val_heads = values.reshape(TOKENS, KV, HD)
    key_padded = jnp.pad(k_rot, ((WINDOW, 0), (0, 0), (0, 0)))
    val_padded = jnp.pad(val_heads, ((WINDOW, 0), (0, 0), (0, 0)))

    def block(block_index):
        first_row = (block_index * TOK_DEV).astype(jnp.int32)
        query_block = lax.dynamic_slice_in_dim(q_rot, first_row, TOK_DEV, 0).reshape(TOK_DEV, KV, group, HD)
        key_block = lax.dynamic_slice_in_dim(key_padded, first_row, WINDOW + TOK_DEV, 0)
        val_block = lax.dynamic_slice_in_dim(val_padded, first_row, WINDOW + TOK_DEV, 0)
        scores = jnp.einsum('tkgd,skd->kgts', query_block.astype(jnp.float32), key_block.astype(jnp.float32)) * query_scale
        query_pos = first_row + jnp.arange(TOK_DEV, dtype=jnp.int32)
        key_pos = first_row - WINDOW + jnp.arange(WINDOW + TOK_DEV, dtype=jnp.int32)
        offsets = query_pos[:, None] - key_pos[None, :]
        allowed = ((key_pos >= 0)[None, :] & (offsets >= 0) & (offsets < WINDOW))[None, None]
        scores = jnp.where(allowed, scores, -1e+30)
        row_max = lax.optimization_barrier(jnp.max(scores, axis=-1, keepdims=True))
        weights = jnp.where(allowed, jnp.exp(scores - row_max), 0.0)
        probs = (weights / lax.optimization_barrier(jnp.sum(weights, axis=-1, keepdims=True))).astype(jnp.bfloat16)
        attended = jnp.einsum('kgts,skd->tkgd', probs.astype(jnp.float32), val_block.astype(jnp.float32)).astype(jnp.bfloat16)
        attended = attended.reshape(TOK_DEV, HEADS * HD)
        hidden = jnp.dot(attended, out_proj, preferred_element_type=jnp.float32)
        inv_rms = lax.rsqrt(lax.optimization_barrier(jnp.mean(hidden * hidden, axis=-1, keepdims=True)) + norm_eps)
        normed = hidden * inv_rms * post_gain[None, :]
        erase_code = jnp.dot(normed - mean_vec[None, :], erase_in, precision=lax.Precision.HIGHEST)
        return (normed - jnp.dot(erase_code, erase_out.T, precision=lax.Precision.HIGHEST)).astype(jnp.bfloat16)
    blocks = lax.map(block, jnp.arange(N_ROW, dtype=jnp.int32))
    return blocks.reshape(TOKENS, D)
```

```python
import functools

import jax
import jax.numpy as jnp
import numpy as np
from jax import lax
from jax.experimental import pallas as pl
from jax.experimental.pallas import tpu as pltpu
from jax.sharding import PartitionSpec as P

HD = 128
WINDOW = 1024
MESH = pl.DeviceIdType.MESH
query_scale = 168.0 ** (-0.5)
norm_eps = 1e-06
rope_base = 10000.0
QB = 256
TN = 384
BIG = 1e30


def split_cat(x):
    hi = x.astype(jnp.bfloat16).astype(jnp.float32)
    return jnp.concatenate([hi, x - hi], axis=1).astype(jnp.bfloat16)


def hi_lo(x):
    hi = x.astype(jnp.bfloat16)
    return hi, (x - hi.astype(jnp.float32)).astype(jnp.bfloat16)


def kernel(n_row, d_full, q_hbm, k_hbm, v_hbm, w_hbm, gain_ref, mean_ref, ein_ref, eout_ref, inv_ref,
           out_ref, qbuf, kbuf, vbuf, krot, wbuf, att, hidden, cosb, sinb, ein_cat, eout_cat,
           st_send, st_recv, loc_sem, wr_sem, ws_sem, kr_sem, ks_sem, as_sem, ar_sem, ss_sem, sr_sem):
    nz = n_row // 2
    g, r, f = lax.axis_index("grp"), lax.axis_index("row"), lax.axis_index("col")
    zz, yy = r // 2, r % 2
    has_up, has_dn = zz < nz - 1, zz > 0
    tok = qbuf.shape[0]
    rows, half = wbuf.shape[1], wbuf.shape[2]
    heads = qbuf.shape[1] // HD
    kvh = kbuf.shape[2] // HD
    acols = heads * HD
    n_tile = half // TN

    part = {"grp": g, "row": r, "col": 1 - f}
    xnb = {"grp": 1 - g, "row": r, "col": f}
    ynb = {"grp": g, "row": 2 * zz + 1 - yy, "col": f}
    up = {"grp": g, "row": r + 2, "col": f}
    dn = {"grp": g, "row": r - 2, "col": f}

    barrier = pltpu.get_barrier_semaphore()
    for nb in (part, xnb, ynb):
        pl.semaphore_signal(barrier, inc=1, device_id=nb, device_id_type=MESH)

    @pl.when(has_up)
    def _():
        pl.semaphore_signal(barrier, inc=1, device_id=up, device_id_type=MESH)

    @pl.when(has_dn)
    def _():
        pl.semaphore_signal(barrier, inc=1, device_id=dn, device_id_type=MESH)

    u_own = f * n_row + r
    loc = [
        pltpu.make_async_copy(w_hbm.at[:, pl.ds(pl.multiple_of(f * half, 128), half)], wbuf.at[u_own], loc_sem.at[0]),
        pltpu.make_async_copy(k_hbm, kbuf.at[2], loc_sem.at[1]),
        pltpu.make_async_copy(q_hbm, qbuf, loc_sem.at[2]),
        pltpu.make_async_copy(v_hbm, vbuf.at[2], loc_sem.at[3]),
    ]
    for c in loc:
        c.start()

    pl.semaphore_wait(barrier, 3 + has_up.astype(jnp.int32) + has_dn.astype(jnp.int32))

    pending = []

    def send(cond, make):
        pending.append((cond, make))
        if cond is None:
            make().start()
        else:
            @pl.when(cond)
            def _():
                make().start()

    n_ws = [0]

    def send_w(cond, u, dev, src=None):
        i = n_ws[0]
        n_ws[0] += 1

        def make():
            return pltpu.make_async_remote_copy(
                src_ref=wbuf.at[u] if src is None else src(), dst_ref=wbuf.at[u],
                send_sem=ws_sem.at[i], recv_sem=wr_sem.at[u], device_id=dev, device_id_type=MESH)

        send(cond, make)

    n_ks = [0]

    def send_kv(cond, src, buf, slot, which, dev):
        i = n_ks[0]
        n_ks[0] += 1

        def make():
            return pltpu.make_async_remote_copy(
                src_ref=src(), dst_ref=buf.at[slot], send_sem=ks_sem.at[i],
                recv_sem=kr_sem.at[2 * slot + which], device_id=dev, device_id_type=MESH)

        send(cond, make)

    def wait_w(u):
        pltpu.make_async_copy(wbuf.at[u], wbuf.at[u], wr_sem.at[u]).wait()

    def wait_kv(slot):
        pltpu.make_async_copy(kbuf.at[slot], kbuf.at[slot], kr_sem.at[2 * slot]).wait()
        pltpu.make_async_copy(vbuf.at[slot], vbuf.at[slot], kr_sem.at[2 * slot + 1]).wait()

    send_w(None, u_own, part, lambda: w_hbm.at[:, pl.ds(pl.multiple_of((1 - f) * half, 128), half)])
    send_kv(yy == 0, lambda: k_hbm, kbuf, 1, 0, ynb)
    send_kv(yy == 0, lambda: v_hbm, vbuf, 1, 1, ynb)
    send_kv(has_up, lambda: k_hbm, kbuf, 0, 0, up)

    def unit(c, z, y):
        return c * n_row + 2 * z + y

    u_line = unit(g, zz, yy)
    u_other = unit(1 - g, zz, yy)
    loc[0].wait()
    wait_w(unit(1 - f, zz, yy))
    send_w(has_up, u_line, up)
    send_w(has_dn, u_line, dn)
    send_kv(has_up, lambda: v_hbm, vbuf, 0, 1, up)
    send_w(None, u_line, ynb)

    @pl.when(zz == 0)
    def _():
        kbuf[0] = jnp.zeros(kbuf.shape[1:], kbuf.dtype)
        vbuf[0] = jnp.zeros(vbuf.shape[1:], vbuf.dtype)

    @pl.when(r == 0)
    def _():
        kbuf[1] = jnp.zeros(kbuf.shape[1:], kbuf.dtype)
        vbuf[1] = jnp.zeros(vbuf.shape[1:], vbuf.dtype)

    sign = jnp.where(lax.broadcasted_iota(jnp.int32, (1, HD), 1) < HD // 2, -1.0, 1.0)
    key_base = r * tok - 2 * tok

    def table(i, _):
        at = pl.multiple_of(i * 128, 128)
        pos = (key_base + at + lax.broadcasted_iota(jnp.int32, (128, HD), 0)).astype(jnp.float32)
        ang = pos * inv_ref[...]
        cosb[pl.ds(at, 128), :] = jnp.cos(ang)
        sinb[pl.ds(at, 128), :] = jnp.sin(ang) * sign
        return 0

    lax.fori_loop(0, 3 * tok // 128, table, 0)

    def turned(x, at):
        x = x.astype(jnp.float32)
        cs, sn = cosb[pl.ds(at, 128), :], sinb[pl.ds(at, 128), :]
        return (x * cs + pltpu.roll(x, HD // 2, 1) * sn).astype(jnp.bfloat16)

    loc[2].wait()

    def rot_q(i, _):
        at = pl.multiple_of(i * 128, 128)
        for h in range(heads):
            cols = slice(h * HD, (h + 1) * HD)
            qbuf[pl.ds(at, 128), cols] = turned(qbuf[pl.ds(at, 128), cols], 2 * tok + at)
        return 0

    lax.fori_loop(0, tok // 128, rot_q, 0)

    def rot_k(slot):
        def body(i, _):
            at = pl.multiple_of(i * 128, 128)
            for h in range(kvh):
                cols = slice(h * HD, (h + 1) * HD)
                krot[pl.ds(slot * tok + at, 128), cols] = turned(kbuf[slot, pl.ds(at, 128), cols], slot * tok + at)
            return 0

        lax.fori_loop(0, tok // 128, body, 0)

    loc[1].wait()
    loc[3].wait()
    rot_k(2)

    def prep(i, _):
        at = pl.multiple_of(i * TN, 128)
        ein_cat[pl.ds(at, TN), :] = split_cat(ein_ref[pl.ds(at, TN), :])
        eout_cat[pl.ds(at, TN), :] = split_cat(eout_ref[pl.ds(at, TN), :])
        return 0

    lax.fori_loop(0, n_tile, prep, 0)

    m_hi, m_lo = hi_lo(jnp.broadcast_to(mean_ref[...], (16, half)))
    m_acc = jnp.dot(m_hi, ein_cat[...], preferred_element_type=jnp.float32) + jnp.dot(
        m_lo, ein_cat[...], preferred_element_type=jnp.float32)
    st_send[tok:tok + 8, :] = (m_acc + pltpu.roll(m_acc, HD // 2, 1))[0:8]

    def z_event(k):
        below, above = zz - k >= 0, zz + k < nz
        for cond, src_z, onward, can in ((below, zz - k, up, has_up), (above, zz + k, dn, has_dn)):
            u = unit(g, src_z, yy)

            @pl.when(cond)
            def _():
                wait_w(u)

            send_w(cond & can, u, onward)
            send_w(cond, u, ynb)
            send_w(cond, u, xnb)

    def d_event(k):
        for cond, src_z in ((zz - k >= 0, zz - k), (zz + k < nz, zz + k)):
            u = unit(g, src_z, 1 - yy)

            @pl.when(cond)
            def _():
                wait_w(u)

            send_w(cond, u, xnb)

    z_event(1)

    @pl.when(zz > 0)
    def _():
        wait_kv(0)

    relay = (zz > 0) & (yy == 1)
    send_kv(relay, lambda: kbuf.at[0], kbuf, 1, 0, ynb)
    send_kv(relay, lambda: vbuf.at[0], vbuf, 1, 1, ynb)
    rot_k(0)
    d_event(1)
    z_event(2)
    send_w(None, u_other, ynb)

    @pl.when(r > 0)
    def _():
        wait_kv(1)

    rot_k(1)

    nt = WINDOW // QB + 1
    ri = lax.broadcasted_iota(jnp.int32, (QB, QB), 0)
    ci = lax.broadcasted_iota(jnp.int32, (QB, QB), 1)
    per = tok // QB
    pen = [jnp.where(zz > 0, 0.0, BIG), jnp.where(r > 0, 0.0, BIG), jnp.float32(0.0)]

    def make_att(p):
        cols = pl.ds(pl.multiple_of(f * acols + p * 2 * HD, 128), 2 * HD)
        return pltpu.make_async_remote_copy(
            src_ref=att.at[:, cols], dst_ref=att.at[:, cols], send_sem=as_sem.at[p], recv_sem=ar_sem.at[p],
            device_id=part, device_id_type=MESH)

    def wait_att(p):
        cols = pl.ds(pl.multiple_of((1 - f) * acols + p * 2 * HD, 128), 2 * HD)
        pltpu.make_async_copy(att.at[:, cols], att.at[:, cols], ar_sem.at[p]).wait()

    def piece(j, _):
        head, i = j // per, j % per
        kv = head // (heads // kvh)
        qt = qbuf[pl.ds(pl.multiple_of(i * QB, QB), QB), pl.ds(pl.multiple_of(head * HD, HD), HD)]
        key_rows = pl.ds(pl.multiple_of(i * QB, QB), nt * QB)
        kv_cols = pl.ds(pl.multiple_of(kv * HD, HD), HD)
        s = lax.dot_general(qt, krot[key_rows, kv_cols], (((1,), (1,)), ((), ())),
                            preferred_element_type=jnp.float32) * query_scale
        tiles, bias, m = [], [], None
        for t in range(nt):
            st = s[:, t * QB:(t + 1) * QB]
            if t == 0:
                st = jnp.where(ci > ri, st, -BIG)
            if t == nt - 1:
                st = jnp.where(ci <= ri, st, -BIG)
            blk = (i + t) // per
            b = jnp.where(blk == 0, pen[0], jnp.where(blk == 1, pen[1], pen[2]))
            mt = jnp.max(st, axis=1, keepdims=True) - b
            m = mt if m is None else jnp.maximum(m, mt)
            tiles.append(st)
            bias.append(b)
        es, tot = [], None
        for st, b in zip(tiles, bias):
            e = jnp.exp(st - (m + b))
            es.append(e)
            se = jnp.sum(e, axis=1, keepdims=True)
            tot = se if tot is None else tot + se
        inv = 1.0 / tot
        p = jnp.concatenate([(e * inv).astype(jnp.bfloat16) for e in es], axis=1)
        o = jnp.dot(p, vflat[key_rows, kv_cols], preferred_element_type=jnp.float32)
        att[pl.ds(pl.multiple_of(i * QB, QB), QB),
            pl.ds(pl.multiple_of(f * acols + head * HD, HD), HD)] = o.astype(jnp.bfloat16)

        for pp in range(heads // 2 - 1):
            @pl.when(j == (2 * pp + 3) * per)
            def _():
                make_att(pp).start()
        return 0

    vflat = vbuf.reshape(3 * tok, kvh * HD)
    n_piece = heads * per
    if nz == 4:
        lax.fori_loop(0, n_piece // 2, piece, 0)
        z_event(3)
        d_event(2)
        lax.fori_loop(n_piece // 2, n_piece, piece, 0)
    else:
        lax.fori_loop(0, n_piece, piece, 0)
    make_att(heads // 2 - 1).start()
    if nz == 4:
        d_event(3)
    else:
        for k in range(3, nz):
            z_event(k)
        for k in range(2, nz):
            d_event(k)

    def mm(first, chunks):
        def body(n, _):
            cols = pl.ds(pl.multiple_of(n * TN, 128), TN)
            acc = None if first else hidden[:, cols]
            for w_at, a_at in chunks:
                cnt = QB // rows
                wt = wbuf[pl.ds(w_at, cnt), :, cols].reshape(QB, TN)
                d = jnp.dot(att[:, pl.ds(pl.multiple_of(a_at, 128), QB)], wt, preferred_element_type=jnp.float32)
                acc = d if acc is None else acc + d
            hidden[:, cols] = acc
            return 0

        lax.fori_loop(0, n_tile, body, 0)

    wait_w(unit(0, zz, 1 - yy))
    wait_w(unit(1, zz, 1 - yy))
    for p in range(heads // 2):
        make_att(p).wait_send()
        wait_att(p)
    if rows == HD:
        def plane(first, z):
            mm(first, [(unit(c, z, 0), unit(c, z, 0) * rows) for c in range(2)])

        plane(True, zz)
        for k in range(1, nz):
            for cond, src_z in ((zz - k >= 0, zz - k), (zz + k < nz, zz + k)):
                @pl.when(cond)
                def _():
                    wait_w(unit(1 - g, src_z, yy))
                    wait_w(unit(1 - g, src_z, 1 - yy))
                    plane(False, src_z)
    else:
        for k in range(1, nz):
            for cond, src_z in ((zz - k >= 0, zz - k), (zz + k < nz, zz + k)):
                @pl.when(cond)
                def _():
                    wait_w(unit(1 - g, src_z, yy))
                    wait_w(unit(1 - g, src_z, 1 - yy))
        cnt = QB // rows
        for c in range(wbuf.shape[0] // cnt):
            mm(c == 0, [(c * cnt, c * QB)])

    lane = lax.broadcasted_iota(jnp.int32, (tok, HD), 1)

    def stats(n, carry):
        code, sq = carry
        cols = pl.ds(pl.multiple_of(n * TN, 128), TN)
        h = hidden[:, cols]
        sq = sq + jnp.sum(h * h, axis=1, keepdims=True)
        hi, lo = hi_lo(h * gain_ref[:, cols])
        e = ein_cat[cols, :]
        code = code + jnp.dot(hi, e, preferred_element_type=jnp.float32) + jnp.dot(
            lo, e, preferred_element_type=jnp.float32)
        return code, sq

    code, sq = lax.fori_loop(0, n_tile, stats, (jnp.zeros((tok, HD), jnp.float32), jnp.zeros((tok, 1), jnp.float32)))
    code = code + pltpu.roll(code, HD // 2, 1)
    st_send[0:tok, :] = jnp.where(lane < HD // 2, code, sq)
    swap = pltpu.make_async_remote_copy(src_ref=st_send, dst_ref=st_recv, send_sem=ss_sem, recv_sem=sr_sem,
                                        device_id=part, device_id_type=MESH)
    swap.start()
    for cond, make in pending:
        if cond is None:
            make().wait_send()
        else:
            @pl.when(cond)
            def _():
                make().wait_send()
    swap.wait()
    both = st_send[0:tok, :] + st_recv[0:tok, :]
    turned_both = pltpu.roll(both, HD // 2, 1)
    code = jnp.where(lane < HD // 2, both, turned_both)
    total = jnp.where(lane < HD // 2, turned_both, both)
    inv_rms = lax.rsqrt(total * (1.0 / d_full) + norm_eps)
    mean_sum = st_send[tok:tok + 1, :] + st_recv[tok:tok + 1, :]
    c_hi, c_lo = hi_lo(inv_rms * code - mean_sum)
    scale = inv_rms[:, 0:1]

    def finish(n, _):
        cols = pl.ds(pl.multiple_of(n * TN, 128), TN)
        e = eout_cat[cols, :]
        nt_dims = (((1,), (1,)), ((), ()))
        back = lax.dot_general(c_hi, e, nt_dims, preferred_element_type=jnp.float32) + lax.dot_general(
            c_lo, e, nt_dims, preferred_element_type=jnp.float32)
        out_ref[:, cols] = (hidden[:, cols] * scale * gain_ref[:, cols] - back).astype(jnp.bfloat16)
        return 0

    lax.fori_loop(0, n_tile, finish, 0)


def solution(mesh):
    n_row = mesh.shape["row"]

    def on_device(queries, keys, values, out_proj, post_gain, mean_vec, erase_in, erase_out):
        tok = queries.shape[0]
        rows, d_full = out_proj.shape
        half = post_gain.shape[0]
        n_unit = 2 * n_row
        nz = n_row // 2
        half_dim = HD // 2
        inverse = np.exp(-(2.0 * np.arange(half_dim, dtype=np.float32) / HD) * np.log(np.float32(rope_base)))
        inverse = np.concatenate([inverse, inverse]).astype(np.float32)[None, :]
        any_spec = pl.BlockSpec(memory_space=pl.ANY)
        vm = pl.BlockSpec(memory_space=pltpu.VMEM)
        n_ws = 5 + 8 * (nz - 1) + 4
        bf, f32 = jnp.bfloat16, jnp.float32
        dma = pltpu.SemaphoreType.DMA
        return pl.pallas_call(
            functools.partial(kernel, n_row, d_full),
            out_shape=jax.ShapeDtypeStruct((tok, half), bf),
            in_specs=[any_spec] * 4 + [vm] * 5,
            out_specs=vm,
            scratch_shapes=[
                pltpu.VMEM(queries.shape, bf),
                pltpu.VMEM((3,) + keys.shape, bf),
                pltpu.VMEM((3,) + keys.shape, bf),
                pltpu.VMEM((3 * tok, keys.shape[1]), bf),
                pltpu.VMEM((n_unit, rows, half), bf),
                pltpu.VMEM((tok, 2 * queries.shape[1]), bf),
                pltpu.VMEM((tok, half), f32),
                pltpu.VMEM((3 * tok, HD), f32),
                pltpu.VMEM((3 * tok, HD), f32),
                pltpu.VMEM((half, HD), bf),
                pltpu.VMEM((half, HD), bf),
                pltpu.VMEM((tok + 8, HD), f32),
                pltpu.VMEM((tok + 8, HD), f32),
                dma((4,)), dma((n_unit,)), dma((n_ws,)), dma((4,)), dma((6,)),
                dma((4,)), dma((4,)), dma, dma,
            ],
            compiler_params=pltpu.CompilerParams(
                collective_id=0, has_side_effects=True, vmem_limit_bytes=60 * 1024 * 1024),
        )(queries, keys, values, out_proj, post_gain.reshape(1, -1), mean_vec.reshape(1, -1),
          erase_in, erase_out, jnp.asarray(inverse))

    placed = (
        P(("grp", "row"), "col"),
        P(("grp", "row"), "col"),
        P(("grp", "row"), "col"),
        P(("col", "row"), None),
        P("col"),
        P("col"),
        P("col", None),
        P("col", None),
    )
    return jax.shard_map(
        on_device, mesh=mesh, in_specs=placed, out_specs=P(("grp", "row"), "col"), check_vma=False
    )
```

```python
import functools

import jax
import jax.numpy as jnp
import numpy as np
from jax import lax
from jax.experimental import pallas as pl
from jax.experimental.pallas import tpu as pltpu
from jax.sharding import PartitionSpec as P

HD = 128
WINDOW = 1024
MESH = pl.DeviceIdType.MESH
query_scale = 168.0 ** (-0.5)
norm_eps = 1e-06
rope_base = 10000.0
QB = 256
TN = 384
BIG = 1e30


def split_cat(x):
    hi = x.astype(jnp.bfloat16).astype(jnp.float32)
    return jnp.concatenate([hi, x - hi], axis=0).astype(jnp.bfloat16)


def hi_lo(x):
    hi = x.astype(jnp.bfloat16)
    return hi, (x - hi.astype(jnp.float32)).astype(jnp.bfloat16)


def dot_nt(x, y):
    return lax.dot_general(x, y, (((1,), (1,)), ((), ())), preferred_element_type=jnp.float32)


def kernel(n_row, d_full, parts, q_hbm, k_hbm, v_hbm, w_hbm, gain_ref, mean_ref, ein_ref, eout_ref, inv_ref,
           out_ref, qbuf, kbuf, vbuf, krot, wbuf, att, hidden, cosb, sinb, ein_cat, eout_cat,
           st_send, st_recv, loc_sem, wr_sem, ws_sem, kr_sem, ks_sem, as_sem, ar_sem, ss_sem, sr_sem):
    nz = n_row // 2
    g, r, f = lax.axis_index("grp"), lax.axis_index("row"), lax.axis_index("col")
    zz, yy = r // 2, r % 2
    has_up, has_dn = zz < nz - 1, zz > 0
    tok = qbuf.shape[0]
    sub, half = wbuf.shape[1], wbuf.shape[2]
    rows = sub * parts
    heads = qbuf.shape[1] // HD
    kvh = kbuf.shape[2] // HD
    acols = heads * HD
    n_tile = half // TN

    part = {"grp": g, "row": r, "col": 1 - f}
    xnb = {"grp": 1 - g, "row": r, "col": f}
    ynb = {"grp": g, "row": 2 * zz + 1 - yy, "col": f}
    up = {"grp": g, "row": r + 2, "col": f}
    dn = {"grp": g, "row": r - 2, "col": f}

    barrier = pltpu.get_barrier_semaphore()
    for nb in (part, xnb, ynb):
        pl.semaphore_signal(barrier, inc=1, device_id=nb, device_id_type=MESH)

    @pl.when(has_up)
    def _():
        pl.semaphore_signal(barrier, inc=1, device_id=up, device_id_type=MESH)

    @pl.when(has_dn)
    def _():
        pl.semaphore_signal(barrier, inc=1, device_id=dn, device_id_type=MESH)

    u_own = f * n_row + r

    def own_w(s, c):
        return w_hbm.at[pl.ds(s * sub, sub), pl.ds(pl.multiple_of(c * half, 128), half)]

    loc_w = [pltpu.make_async_copy(own_w(s, f), wbuf.at[u_own * parts + s], loc_sem.at[3 + s]) for s in range(parts)]
    loc = loc_w + [
        pltpu.make_async_copy(k_hbm, kbuf.at[2], loc_sem.at[0]),
        pltpu.make_async_copy(q_hbm, qbuf, loc_sem.at[1]),
        pltpu.make_async_copy(v_hbm, vbuf.at[2], loc_sem.at[2]),
    ]
    for c in loc:
        c.start()

    pl.semaphore_wait(barrier, 3 + has_up.astype(jnp.int32) + has_dn.astype(jnp.int32))

    pending = []

    def send(cond, make):
        pending.append((cond, make))
        if cond is None:
            make().start()
        else:
            @pl.when(cond)
            def _():
                make().start()

    n_ws = [0]

    def send_w(cond, u, s, dev, src=None):
        i = n_ws[0]
        n_ws[0] += 1

        def make():
            slot = u * parts + s
            return pltpu.make_async_remote_copy(
                src_ref=wbuf.at[slot] if src is None else src(), dst_ref=wbuf.at[slot],
                send_sem=ws_sem.at[i], recv_sem=wr_sem.at[slot], device_id=dev, device_id_type=MESH)

        send(cond, make)

    n_ks = [0]

    def send_kv(cond, src, buf, slot, which, dev):
        i = n_ks[0]
        n_ks[0] += 1

        def make():
            return pltpu.make_async_remote_copy(
                src_ref=src(), dst_ref=buf.at[slot], send_sem=ks_sem.at[i],
                recv_sem=kr_sem.at[2 * slot + which], device_id=dev, device_id_type=MESH)

        send(cond, make)

    def wait_w(u, s):
        slot = u * parts + s
        pltpu.make_async_copy(wbuf.at[slot], wbuf.at[slot], wr_sem.at[slot]).wait()

    every = range(parts)

    def wait_kv(slot):
        pltpu.make_async_copy(kbuf.at[slot], kbuf.at[slot], kr_sem.at[2 * slot]).wait()
        pltpu.make_async_copy(vbuf.at[slot], vbuf.at[slot], kr_sem.at[2 * slot + 1]).wait()

    for s in every:
        send_w(None, u_own, s, part, lambda s=s: own_w(s, 1 - f))

    def unit(c, z, y):
        return c * n_row + 2 * z + y

    u_line = unit(g, zz, yy)
    for s in every:
        loc_w[s].wait()
        wait_w(unit(1 - f, zz, yy), s)
        send_w(has_up, u_line, s, up)
        send_w(has_dn, u_line, s, dn)
        send_w(None, u_line, s, ynb)
    send_kv(has_up, lambda: k_hbm, kbuf, 0, 0, up)
    send_kv(has_up, lambda: v_hbm, vbuf, 0, 1, up)

    @pl.when(zz == 0)
    def _():
        kbuf[0] = jnp.zeros(kbuf.shape[1:], kbuf.dtype)
        vbuf[0] = jnp.zeros(vbuf.shape[1:], vbuf.dtype)

    @pl.when(r == 0)
    def _():
        kbuf[1] = jnp.zeros(kbuf.shape[1:], kbuf.dtype)
        vbuf[1] = jnp.zeros(vbuf.shape[1:], vbuf.dtype)

    sign = jnp.where(lax.broadcasted_iota(jnp.int32, (1, HD), 1) < HD // 2, -1.0, 1.0)
    key_base = r * tok - 2 * tok

    def table(i, _):
        at = pl.multiple_of(i * 128, 128)
        pos = (key_base + at + lax.broadcasted_iota(jnp.int32, (128, HD), 0)).astype(jnp.float32)
        ang = pos * inv_ref[...]
        cosb[pl.ds(at, 128), :] = jnp.cos(ang)
        sinb[pl.ds(at, 128), :] = jnp.sin(ang) * sign
        return 0

    lax.fori_loop(0, 3 * tok // 128, table, 0)

    def turned(x, at):
        x = x.astype(jnp.float32)
        cs, sn = cosb[pl.ds(at, 128), :], sinb[pl.ds(at, 128), :]
        return (x * cs + pltpu.roll(x, HD // 2, 1) * sn).astype(jnp.bfloat16)

    loc[parts + 1].wait()

    def rot_q(i, _):
        at = pl.multiple_of(i * 128, 128)
        for h in range(heads):
            cols = slice(h * HD, (h + 1) * HD)
            qbuf[pl.ds(at, 128), cols] = turned(qbuf[pl.ds(at, 128), cols], 2 * tok + at)
        return 0

    lax.fori_loop(0, tok // 128, rot_q, 0)

    def rot_k(slot):
        def body(i, _):
            at = pl.multiple_of(i * 128, 128)
            for h in range(kvh):
                cols = slice(h * HD, (h + 1) * HD)
                krot[pl.ds(slot * tok + at, 128), cols] = turned(kbuf[slot, pl.ds(at, 128), cols], slot * tok + at)
            return 0

        lax.fori_loop(0, tok // 128, body, 0)

    loc[parts].wait()
    loc[parts + 2].wait()
    rot_k(2)

    def prep(i, _):
        at = pl.multiple_of(i * TN, 128)
        ein_cat[:, pl.ds(at, TN)] = split_cat(ein_ref[:, pl.ds(at, TN)])
        eout_cat[:, pl.ds(at, TN)] = split_cat(eout_ref[:, pl.ds(at, TN)])
        return 0

    lax.fori_loop(0, n_tile, prep, 0)

    m_hi, m_lo = hi_lo(jnp.broadcast_to(mean_ref[...][None, :], (16, half)))
    m_acc = dot_nt(m_hi, ein_cat[...]) + dot_nt(m_lo, ein_cat[...])
    st_send[tok:tok + 8, :] = (m_acc + pltpu.roll(m_acc, HD // 2, 1))[0:8]

    def side(cond, z, onward, can):
        return cond, cond & can, z, onward, unit(g, z, yy), unit(g, z, 1 - yy), unit(1 - g, z, yy)

    near = [None] + [
        (side(zz - k >= 0, zz - k, up, has_up), side(zz + k < nz, zz + k, dn, has_dn)) for k in range(1, nz)
    ]

    def z_event(k, s):
        for cond, further, _, onward, u, _, _ in near[k]:
            @pl.when(cond)
            def _():
                wait_w(u, s)

            if k < nz - 1:
                send_w(further, u, s, onward)
            send_w(cond, u, s, ynb)
            send_w(cond, u, s, xnb)

    def by_y(k, s):
        return parts > 1 and s >= parts // 2 and k in (nz - 1, nz - 2)

    def d_event(k, s):
        for cond, _, _, _, _, u_y, u_x in near[k]:
            u = u_x if by_y(k, s) else u_y

            @pl.when(cond)
            def _():
                wait_w(u, s)

            send_w(cond, u, s, ynb if by_y(k, s) else xnb)

    def own_to_x(s):
        u = unit(g, zz, 1 - yy)
        wait_w(u, s)
        send_w(None, u, s, xnb)

    for s in every:
        z_event(1, s)
        own_to_x(s)
    send_kv(yy == 0, lambda: k_hbm, kbuf, 1, 0, ynb)
    send_kv(yy == 0, lambda: v_hbm, vbuf, 1, 1, ynb)
    for s in every:
        d_event(1, s)

    @pl.when(zz > 0)
    def _():
        wait_kv(0)

    relay = (zz > 0) & (yy == 1)
    send_kv(relay, lambda: kbuf.at[0], kbuf, 1, 0, ynb)
    send_kv(relay, lambda: vbuf.at[0], vbuf, 1, 1, ynb)
    rot_k(0)
    for s in every:
        z_event(2, s)
    if nz == 4:
        for s in range(parts // 2):
            z_event(3, s)

    @pl.when(r > 0)
    def _():
        wait_kv(1)

    rot_k(1)

    nt = WINDOW // QB + 1
    ri = lax.broadcasted_iota(jnp.int32, (QB, QB), 0)
    ci = lax.broadcasted_iota(jnp.int32, (QB, QB), 1)
    per = tok // QB
    pen = [jnp.where(zz > 0, 0.0, BIG), jnp.where(r > 0, 0.0, BIG), jnp.float32(0.0)]

    def make_att(p):
        cols = pl.ds(pl.multiple_of(f * acols + p * 2 * HD, 128), 2 * HD)
        return pltpu.make_async_remote_copy(
            src_ref=att.at[:, cols], dst_ref=att.at[:, cols], send_sem=as_sem.at[p], recv_sem=ar_sem.at[p],
            device_id=part, device_id_type=MESH)

    def wait_att(p):
        cols = pl.ds(pl.multiple_of((1 - f) * acols + p * 2 * HD, 128), 2 * HD)
        pltpu.make_async_copy(att.at[:, cols], att.at[:, cols], ar_sem.at[p]).wait()

    def piece(j, _):
        head, i = j // per, j % per
        kv = head // (heads // kvh)
        qt = qbuf[pl.ds(pl.multiple_of(i * QB, QB), QB), pl.ds(pl.multiple_of(head * HD, HD), HD)]
        key_rows = pl.ds(pl.multiple_of(i * QB, QB), nt * QB)
        kv_cols = pl.ds(pl.multiple_of(kv * HD, HD), HD)
        s = dot_nt(qt, krot[key_rows, kv_cols]) * query_scale
        tiles, bias, m = [], [], None
        for t in range(nt):
            st = s[:, t * QB:(t + 1) * QB]
            if t == 0:
                st = jnp.where(ci > ri, st, -BIG)
            if t == nt - 1:
                st = jnp.where(ci <= ri, st, -BIG)
            blk = (i + t) // per
            b = jnp.where(blk == 0, pen[0], jnp.where(blk == 1, pen[1], pen[2]))
            mt = jnp.max(st, axis=1, keepdims=True) - b
            m = mt if m is None else jnp.maximum(m, mt)
            tiles.append(st)
            bias.append(b)
        es, tot = [], None
        for st, b in zip(tiles, bias):
            e = jnp.exp(st - (m + b))
            es.append(e)
            se = jnp.sum(e, axis=1, keepdims=True)
            tot = se if tot is None else tot + se
        inv = 1.0 / tot
        p = jnp.concatenate([(e * inv).astype(jnp.bfloat16) for e in es], axis=1)
        o = jnp.dot(p, vflat[key_rows, kv_cols], preferred_element_type=jnp.float32)
        att[pl.ds(pl.multiple_of(i * QB, QB), QB),
            pl.ds(pl.multiple_of(f * acols + head * HD, HD), HD)] = o.astype(jnp.bfloat16)

        for pp in range(heads // 2 - 1):
            @pl.when(j == (2 * pp + 3) * per)
            def _():
                make_att(pp).start()
        return 0

    vflat = vbuf.reshape(3 * tok, kvh * HD)
    n_piece = heads * per
    if nz == 4:
        late = [(z_event, 3, s) for s in range(parts // 2, parts)] + [(d_event, k, s) for k in (2, 3) for s in every]
        inside = late
    else:
        late = [(d_event, 2, s) for s in every]
        for k in range(3, nz):
            late += [(z_event, k, s) for s in every] + [(d_event, k, s) for s in every]
        inside = []

    def steps(j, _):
        piece(j, 0)
        for n, (event, k, s) in enumerate(inside):
            @pl.when(j == 1 + (3 * n) // 2)
            def _():
                event(k, s)
        return 0

    lax.fori_loop(0, n_piece, steps, 0)
    make_att(heads // 2 - 1).start()
    for event, k, s in late[len(inside):]:
        event(k, s)

    def mm(first, chunks):
        def body(n, _):
            cols = pl.ds(pl.multiple_of(n * TN, 128), TN)
            acc = None if first else hidden[:, cols]
            for w_at, a_at in chunks:
                cnt = QB // sub
                wt = wbuf[pl.ds(w_at, cnt), :, cols].reshape(QB, TN)
                d = jnp.dot(att[:, pl.ds(pl.multiple_of(a_at, 128), QB)], wt, preferred_element_type=jnp.float32)
                acc = d if acc is None else acc + d
            hidden[:, cols] = acc
            return 0

        lax.fori_loop(0, n_tile, body, 0)

    for s in every:
        wait_w(unit(1 - g, zz, 1 - yy), s)
    for p in range(heads // 2):
        make_att(p).wait_send()
        wait_att(p)

    def wait_rest(k, z):
        for s in every:
            wait_w(unit(1 - g, z, 1 - yy), s)
            wait_w(unit(g, z, 1 - yy) if by_y(k, s) else unit(1 - g, z, yy), s)

    if rows == HD:
        def plane(first, z):
            mm(first, [(unit(c, z, 0) * parts, unit(c, z, 0) * rows) for c in range(2)])

        plane(True, zz)
        for k in range(1, nz):
            for cond, _, z, _, _, _, _ in near[k]:
                @pl.when(cond)
                def _():
                    wait_rest(k, z)
                    plane(False, z)
    else:
        for k in range(1, nz):
            for cond, _, z, _, _, _, _ in near[k]:
                @pl.when(cond)
                def _():
                    wait_rest(k, z)
        cnt = QB // sub
        for c in range(wbuf.shape[0] // cnt):
            mm(c == 0, [(c * cnt, c * QB)])

    lane = lax.broadcasted_iota(jnp.int32, (tok, HD), 1)

    def stats(n, carry):
        code, sq = carry
        cols = pl.ds(pl.multiple_of(n * TN, 128), TN)
        h = hidden[:, cols]
        sq = sq + jnp.sum(h * h, axis=1, keepdims=True)
        hi, lo = hi_lo(h * gain_ref[cols][None, :])
        e = ein_cat[:, cols]
        code = code + dot_nt(hi, e) + dot_nt(lo, e)
        return code, sq

    code, sq = lax.fori_loop(0, n_tile, stats, (jnp.zeros((tok, HD), jnp.float32), jnp.zeros((tok, 1), jnp.float32)))
    code = code + pltpu.roll(code, HD // 2, 1)
    st_send[0:tok, :] = jnp.where(lane < HD // 2, code, sq)
    swap = pltpu.make_async_remote_copy(src_ref=st_send, dst_ref=st_recv, send_sem=ss_sem, recv_sem=sr_sem,
                                        device_id=part, device_id_type=MESH)
    swap.start()
    for cond, make in pending:
        if cond is None:
            make().wait_send()
        else:
            @pl.when(cond)
            def _():
                make().wait_send()
    swap.wait()
    both = st_send[0:tok, :] + st_recv[0:tok, :]
    turned_both = pltpu.roll(both, HD // 2, 1)
    code = jnp.where(lane < HD // 2, both, turned_both)
    total = jnp.where(lane < HD // 2, turned_both, both)
    inv_rms = lax.rsqrt(total * (1.0 / d_full) + norm_eps)
    mean_sum = st_send[tok:tok + 1, :] + st_recv[tok:tok + 1, :]
    c_hi, c_lo = hi_lo(inv_rms * code - mean_sum)
    scale = inv_rms[:, 0:1]

    def finish(n, _):
        cols = pl.ds(pl.multiple_of(n * TN, 128), TN)
        e = eout_cat[:, cols]
        back = jnp.dot(c_hi, e, preferred_element_type=jnp.float32) + jnp.dot(
            c_lo, e, preferred_element_type=jnp.float32)
        out_ref[:, cols] = (hidden[:, cols] * scale * gain_ref[cols][None, :] - back).astype(jnp.bfloat16)
        return 0

    lax.fori_loop(0, n_tile, finish, 0)


def solution(mesh):
    n_row = mesh.shape["row"]

    def on_device(queries, keys, values, out_proj, post_gain, mean_vec, erase_in, erase_out):
        tok = queries.shape[0]
        rows, d_full = out_proj.shape
        half = post_gain.shape[0]
        n_unit = 2 * n_row
        nz = n_row // 2
        half_dim = HD // 2
        inverse = np.exp(-(2.0 * np.arange(half_dim, dtype=np.float32) / HD) * np.log(np.float32(rope_base)))
        inverse = np.concatenate([inverse, inverse]).astype(np.float32)[None, :]
        any_spec = pl.BlockSpec(memory_space=pl.ANY)
        vm = pl.BlockSpec(memory_space=pltpu.VMEM)
        parts = 4 if rows >= 64 else 1
        n_ws = parts * (8 + 8 * nz)
        bf, f32 = jnp.bfloat16, jnp.float32
        dma = pltpu.SemaphoreType.DMA
        return pl.pallas_call(
            functools.partial(kernel, n_row, d_full, parts),
            out_shape=jax.ShapeDtypeStruct((tok, half), bf),
            in_specs=[any_spec] * 4 + [vm] * 5,
            out_specs=vm,
            scratch_shapes=[
                pltpu.VMEM(queries.shape, bf),
                pltpu.VMEM((3,) + keys.shape, bf),
                pltpu.VMEM((3,) + keys.shape, bf),
                pltpu.VMEM((3 * tok, keys.shape[1]), bf),
                pltpu.VMEM((n_unit * parts, rows // parts, half), bf),
                pltpu.VMEM((tok, 2 * queries.shape[1]), bf),
                pltpu.VMEM((tok, half), f32),
                pltpu.VMEM((3 * tok, HD), f32),
                pltpu.VMEM((3 * tok, HD), f32),
                pltpu.VMEM((HD, half), bf),
                pltpu.VMEM((HD, half), bf),
                pltpu.VMEM((tok + 8, HD), f32),
                pltpu.VMEM((tok + 8, HD), f32),
                dma((3 + parts,)), dma((n_unit * parts,)), dma((n_ws,)), dma((4,)), dma((6,)),
                dma((4,)), dma((4,)), dma, dma,
            ],
            compiler_params=pltpu.CompilerParams(
                collective_id=0, has_side_effects=True, vmem_limit_bytes=60 * 1024 * 1024),
        )(queries, keys, values, out_proj, post_gain, mean_vec,
          erase_in.T, erase_out.T, jnp.asarray(inverse))

    placed = (
        P(("grp", "row"), "col"),
        P(("grp", "row"), "col"),
        P(("grp", "row"), "col"),
        P(("col", "row"), None),
        P("col"),
        P("col"),
        P("col", None),
        P("col", None),
    )
    return jax.shard_map(
        on_device, mesh=mesh, in_specs=placed, out_specs=P(("grp", "row"), "col"), check_vma=False
    )
```
